256 devices in a mesh: wide: 32 (over y, x, core), narrow: 8 (over z).
Axes of the slice: x: 4, y: 4, z: 8, core: 2. Of those that a mesh axis runs over, the one named last changes fastest.
Arguments:
- features: bfloat16 [1024, 16384], P('wide', 'narrow'), may hold values from -6 to 6
- queries: bfloat16 [2048, 16384], P('wide', 'narrow'), may hold values from -6 to 6
- damping: float32 [16384], P('wide'), may hold values from 0.25 to 4
Outputs:
- kernel: float32 [16384, 16384], P('wide', 'narrow')
- factor: float32 [16384, 256], P('wide')
- scores: float32 [2048, 1024], P('wide', 'narrow')
The draws below stay inside these ranges and needn't reach their ends.
All inputs are finite; a program needn't handle non-finite values.
Results may differ from the reference program's by a relative error of at most 0.0003.
Values may be sent and summed in bfloat16 or wider, within the bound.
A program may use at most 64 MiB of HBM per device.

```python
import math
import jax
import jax.numpy as jnp
from jax import lax

P_SIZE = 16384
PANEL = 128
PANELS = 2
SLAB = 1024
QUERIES = 2048


def level_of(own_key, shape, split, low, top_value):
    def one(position, parts):
        heights = jax.random.uniform(jax.random.fold_in(jax.random.fold_in(own_key, 6), position), (parts,), jnp.float32, low / len(split), top_value / len(split))
        return jnp.repeat(jnp.exp(heights), shape[position] // parts).reshape((-1,) + (1,) * (len(shape) - position - 1))

    loudness = one(*split[0])
    for cut in split[1:]:
        loudness = loudness * one(*cut)
    return loudness


def noise(own_key, dims, deviation, most, cuts=(), kind=jnp.bfloat16):
    factor_of = level_of(own_key, dims, cuts, -0.22, 0.18) if cuts else 1.0
    entries = jax.random.normal(own_key, dims, jnp.float32) * deviation * factor_of
    return jnp.minimum(jnp.maximum(entries, -most), most).astype(kind)


def setup_inputs(seed: int = 0) -> dict:
    streams_of = jax.random.split(jax.random.key(seed), 4)
    features = noise(streams_of[0], (SLAB, P_SIZE), 1.0, 6.0, ((0, 32), (1, 8)))
    queries = noise(streams_of[1], (QUERIES, P_SIZE), 1.0, 6.0, ((0, 32), (1, 8)))
    damping = jnp.clip(jnp.exp(math.log(4.0) - 2.7725887 * jax.random.uniform(streams_of[2], (P_SIZE,), jnp.float32) ** level_of(streams_of[2], (P_SIZE,), ((0, 32),), -0.2, 0.2)), 0.25, 4.0)
    return dict(features=features, queries=queries, damping=damping)


def reference(features, queries, damping):
    products = lax.dot_general(features.astype(jnp.float32), features.astype(jnp.float32), (((0,), (0,)), ((), ())), preferred_element_type=jnp.float32)
    index_all = jnp.arange(P_SIZE, dtype=jnp.int32)
    kernel = products / SLAB
    kernel = kernel.at[index_all, index_all].add(damping)
    factors = []
    for panel_index in range(PANELS):
        offset = panel_index * PANEL
        pivot_block = kernel[offset:offset + PANEL, offset:offset + PANEL]
        pivot_factor = jnp.linalg.cholesky(pivot_block)
        columns = kernel[:, offset:offset + PANEL]
        lower_rows = lax.linalg.triangular_solve(pivot_factor, columns, left_side=False, lower=True, transpose_a=True)
        kernel = kernel - jnp.dot(lower_rows.astype(jnp.float32), lower_rows.T.astype(jnp.float32), precision=lax.Precision.HIGHEST, preferred_element_type=jnp.float32)
        finished = index_all < offset + PANEL
        kernel = jnp.where(finished[:, None] | finished[None, :], jnp.zeros_like(kernel), kernel)
        factors.append(lower_rows)
    scores = lax.dot_general(queries.astype(jnp.float32), features.astype(jnp.float32), (((1,), (1,)), ((), ())), preferred_element_type=jnp.float32)
    scores = scores * (1.0 / math.sqrt(P_SIZE))
    return (kernel, jnp.concatenate(factors, axis=1), scores)
```

```python
import functools
import math

import jax
import jax.numpy as jnp
from jax import lax
from jax.experimental import pallas as pl
from jax.experimental.pallas import tpu as pltpu
from jax.sharding import PartitionSpec as P

P_SIZE = 16384
PIV = 256
SLAB = 1024
MESH = pl.DeviceIdType.MESH
F32 = jnp.float32
BF16 = jnp.bfloat16

ORDER = (
    (0, 0), (3, 0), (1, 0), (0, 3), (0, 1), (2, 0), (3, 3), (1, 3),
    (3, 1), (1, 1), (2, 3), (2, 1), (0, 2), (3, 2), (1, 2), (2, 2),
)
RELAYED = 10
LAST_STEP = 25


def _table(values, p):
    out = jnp.int32(0)
    for k, v in enumerate(values):
        if v:
            out = out + jnp.where(p == k, jnp.int32(v), jnp.int32(0))
    return out


def gather_kernel(
    feat, qry, damp, fj, fi, fp, dp, sc,
    part, inbox,
    ag_recv, ag_send, pt_recv, pt_send, z_recv, z_send, fpz_recv, fpz_send,
    fp_recv, fp_send, fpp_recv, fpp_send, d_recv, d_send, rs_recv, rs_send, local,
):
    w = lax.axis_index("wide")
    z = lax.axis_index("narrow")
    c = lax.rem(w, 2)
    x = lax.rem(lax.div(w, 2), 4)
    y = lax.div(w, 8)

    def spot(da, db, core):
        px = lax.rem(x + da + core * (db - da), 4)
        py = lax.rem(y + db + core * (da - db), 4)
        return px, py

    def dev(da, db):
        px, py = spot(da, db, c)
        return ((py * 4 + px) * 2 + c, z)

    def row(da, db, core):
        px, py = spot(da, db, core)
        return pl.multiple_of((core * 16 + py * 4 + px) * 32, 32)

    partner = (w + 1 - 2 * c, z)
    own = row(0, 0, c)

    def rcopy(src, dst, ssem, rsem, to):
        return pltpu.make_async_remote_copy(
            src_ref=src, dst_ref=dst, send_sem=ssem, recv_sem=rsem, device_id=to, device_id_type=MESH
        )

    barrier = pltpu.get_barrier_semaphore()

    @pl.loop(1, 32)
    def _(k):
        pl.semaphore_signal(barrier, inc=1, device_id=(lax.rem(w + k, 32), z), device_id_type=MESH)

    @pl.loop(1, 8)
    def _(k):
        pl.semaphore_signal(barrier, inc=1, device_id=(w, lax.rem(z + k, 8)), device_id_type=MESH)

    pl.semaphore_wait(barrier, 38)

    def fpz(k):
        return rcopy(
            feat.at[:, pl.ds(0, PIV)], fp.at[pl.ds(own, 32), :], fpz_send.at[k], fpz_recv,
            (w, lax.rem(z + k, 8)),
        )

    fp_own = pltpu.make_async_copy(feat.at[:, pl.ds(0, PIV)], fp.at[pl.ds(own, 32), :], local.at[0])
    fj_own = pltpu.make_async_copy(feat, fj.at[pl.ds(own, 32), :], local.at[1])
    dp_own = pltpu.make_async_copy(damp, dp, local.at[2])

    def dcopy(k):
        return rcopy(damp, dp, d_send.at[k], d_recv, (lax.rem(w + k, 32), z))

    @pl.when(z == 0)
    def _():
        for k in (4, 3, 5, 2, 6, 1, 7):
            fpz(k).start()
        fp_own.start()

    @pl.when(w == 0)
    def _():
        @pl.loop(1, 32)
        def _(k):
            dcopy(k).start()

        dp_own.start()

    fj_own.start()

    sends = []

    def send_block(da, db, half, to, as_da, as_db, src=None):
        n = len(sends)
        r = row(da, db, c)
        if half is None:
            rows, index = pl.ds(r, 32), (as_da * 4 + as_db) * 2
        else:
            rows, index = pl.ds(r + 16 * half, 16), (as_da * 4 + as_db) * 2 + half
        op = rcopy(
            fj.at[rows, :] if src is None else src, fj.at[rows, :],
            ag_send.at[n], ag_recv.at[index], to,
        )
        op.start()
        sends.append(op)

    def wait_block(da, db):
        r = row(da, db, c)
        base = (da * 4 + db) * 2
        if da == 2 and db == 0 or db == 2:
            for h in range(2):
                ref = fj.at[pl.ds(r + 16 * h, 16), :]
                rcopy(ref, ref, ag_send.at[0], ag_recv.at[base + h], partner).wait_recv()
        else:
            ref = fj.at[pl.ds(r, 32), :]
            rcopy(ref, ref, ag_send.at[0], ag_recv.at[base], partner).wait_recv()

    def to_partner(p):
        da, db = ORDER[p]
        ref = fj.at[pl.ds(row(da, db, c), 32), :]
        op = rcopy(feat if p == 0 else ref, ref, pt_send.at[p], pt_recv.at[p], partner)
        op.start()
        sends.append(op)

    def plane_event(p):
        da, db = ORDER[p]
        src = feat if p == 0 else None
        if p:
            wait_block(da, db)
        if db == 0:
            if da == 0:
                send_block(0, 0, None, dev(1, 0), 3, 0, src)
                send_block(0, 0, None, dev(3, 0), 1, 0, src)
            elif da == 3:
                send_block(3, 0, 0, dev(1, 0), 2, 0)
            elif da == 1:
                send_block(1, 0, 1, dev(3, 0), 2, 0)
            send_block(da, 0, None, dev(0, 1), da, 3, src)
            send_block(da, 0, None, dev(0, 3), da, 1, src)
        elif db == 3:
            send_block(da, 3, 0, dev(0, 1), da, 2)
        elif db == 1:
            send_block(da, 1, 1, dev(0, 3), da, 2)
        to_partner(p)

    def fp_direct(k):
        da, db = lax.div(k, 4), lax.rem(k, 4)
        back = lax.rem(4 - da, 4) * 4 + lax.rem(4 - db, 4)
        ref = fp.at[pl.ds(own, 32), :]
        return rcopy(ref, ref, fp_send.at[k], fp_recv.at[back], dev(da, db))

    half_rows = fp.at[pl.ds(pl.multiple_of(c * 512, 512), 512), :]
    fp_half = rcopy(half_rows, half_rows, fpp_send, fpp_recv, partner)

    def panel_start():
        @pl.when(z == 0)
        def _():
            fp_own.wait()

        @pl.when(z != 0)
        def _():
            fpz(0).wait_recv()

        @pl.loop(1, 16)
        def _(k):
            fp_direct(k).start()

    def panel_to_partner():
        @pl.loop(1, 16)
        def _(k):
            fp_direct(k).wait_recv()

        fp_half.start()

    home = lax.div(w, 4)
    d = lax.rem(z - home + 8, 8)
    sub = pl.multiple_of(lax.rem(w, 4) * 512, 512)
    up = (w, lax.rem(z + 1, 8))
    down = (w, lax.rem(z + 7, 8))
    hops_up = d
    hops_down = lax.rem(8 - d, 8)
    near = jnp.minimum(hops_up, hops_down)

    def z_rows(p, s):
        da = _table([o[0] for o in ORDER], p)
        db = _table([o[1] for o in ORDER], p)
        core = c if s == 0 else 1 - c
        return row(da, db, core)

    def z_copy(p, s, from_root, to, way):
        r = z_rows(p, s)
        dst = fi.at[pl.ds(r, 32), :]
        src = fj.at[pl.ds(r, 32), pl.ds(sub, 512)] if from_root else dst
        q = p * 2 + s
        return rcopy(src, dst, z_send.at[q * 2 + way], z_recv.at[q], to)

    def pt_wait(p):
        ref = fj.at[pl.ds(z_rows(p, 1), 32), :]
        rcopy(ref, ref, pt_send.at[0], pt_recv.at[p], partner).wait_recv()

    def z_step(t):
        first = t - 1

        @pl.when((d == 0) & (first >= 0) & (first < RELAYED))
        def _():
            z_copy(first, 0, True, up, 0).start()
            pt_wait(first)
            z_copy(first, 1, True, down, 1).start()

        @pl.when((d == 0) & (first >= RELAYED) & (first < 16))
        def _():
            z_copy(first, 0, True, up, 0).start()
            z_copy(first, 0, True, down, 1).start()
            pt_wait(first)
            z_copy(first, 1, True, up, 0).start()
            z_copy(first, 1, True, down, 1).start()

        pu = first - 2 * hops_up

        @pl.when((d != 0) & (pu >= 0) & (pu < RELAYED))
        def _():
            z_copy(pu, 0, False, up, 0).wait_recv()

            @pl.when(d < 7)
            def _():
                z_copy(pu, 0, False, up, 0).start()

        pd = first - 2 * hops_down

        @pl.when((d != 0) & (pd >= 0) & (pd < RELAYED))
        def _():
            z_copy(pd, 1, False, down, 1).wait_recv()

            @pl.when(d > 1)
            def _():
                z_copy(pd, 1, False, down, 1).start()

        pn = first - 2 * near

        @pl.when((d != 0) & (pn >= RELAYED) & (pn < 16))
        def _():
            for s in range(2):
                z_copy(pn, s, False, up, 0).wait_recv()

                @pl.when(d < 4)
                def _():
                    z_copy(pn, s, False, up, 0).start()

                @pl.when(d > 5)
                def _():
                    z_copy(pn, s, False, down, 1).start()

    fj_wait = []
    for t in range(16):
        plane_event(t)
        if t == 0:
            fj_own.wait()
        if t == 4:
            panel_start()
        if t == 9:
            panel_to_partner()
        z_step(jnp.int32(t))
    z_step(jnp.int32(16))

    @pl.when(d != 0)
    def _():
        @pl.loop(0, 16)
        def _(p):
            pt_wait(p)

    fi_own = pltpu.make_async_copy(fj.at[:, pl.ds(sub, 512)], fi, local.at[3])

    @pl.when(d == 0)
    def _():
        fi_own.start()

    def scores_for(k):
        yk = lax.div(k, 2)
        xk = lax.rem(k, 2) * 2
        pieces = []
        for dx in range(2):
            for core in range(2):
                r = pl.multiple_of((core * 16 + yk * 4 + xk + dx) * 32, 32)
                pieces.append(fj[pl.ds(r, 32), :])
        return lax.dot_general(
            qry[...], jnp.concatenate(pieces, axis=0), (((1,), (1,)), ((), ())),
            preferred_element_type=F32,
        )

    def rs_copy(k):
        to = lax.rem(z + k, 8)
        return rcopy(part.at[to], inbox.at[k], rs_send.at[k], rs_recv.at[k], (w, to))

    @pl.loop(1, 8)
    def _(k):
        part[lax.rem(z + k, 8)] = scores_for(lax.rem(z + k, 8))
        rs_copy(k).start()

    part[z] = scores_for(z)

    @pl.loop(17, LAST_STEP)
    def _(t):
        z_step(t)

    total = part[z]
    for k in range(1, 8):
        rs_copy(k).wait_recv()
        total = total + inbox[k]
    sc[...] = total * (1.0 / math.sqrt(P_SIZE))

    @pl.when(d == 0)
    def _():
        fi_own.wait()

    fp_half.wait_recv()
    fp_half.wait_send()

    @pl.when(w == 0)
    def _():
        dp_own.wait()

        @pl.loop(1, 32)
        def _(k):
            dcopy(k).wait_send()

    @pl.when(w != 0)
    def _():
        dcopy(0).wait_recv()

    @pl.when(z == 0)
    def _():
        for k in range(1, 8):
            fpz(k).wait_send()

    @pl.loop(1, 16)
    def _(k):
        fp_direct(k).wait_send()

    @pl.loop(1, 8)
    def _(k):
        rs_copy(k).wait_send()

    for op in sends:
        op.wait_send()

    @pl.loop(0, 16)
    def _(p):
        one_way = p < RELAYED

        @pl.when(one_way & (d < 7))
        def _():
            z_copy(p, 0, False, up, 0).wait_send()

        @pl.when(one_way & (d != 1))
        def _():
            z_copy(p, 1, False, down, 1).wait_send()

        for s in range(2):
            @pl.when(jnp.logical_not(one_way) & (d < 4))
            def _():
                z_copy(p, s, False, up, 0).wait_send()

            @pl.when(jnp.logical_not(one_way) & ((d > 5) | (d == 0)))
            def _():
                z_copy(p, s, False, down, 1).wait_send()


def gather(features, queries, damping):
    vmem = pl.BlockSpec(memory_space=pltpu.VMEM)
    dma = pltpu.SemaphoreType.DMA
    return pl.pallas_call(
        gather_kernel,
        name="gather",
        out_shape=[
            jax.ShapeDtypeStruct((SLAB, 2048), BF16),
            jax.ShapeDtypeStruct((SLAB, 512), BF16),
            jax.ShapeDtypeStruct((SLAB, PIV), BF16),
            jax.ShapeDtypeStruct((4, 128), F32),
            jax.ShapeDtypeStruct((64, 128), F32),
        ],
        in_specs=[vmem] * 3,
        out_specs=[vmem] * 5,
        scratch_shapes=[
            pltpu.VMEM((8, 64, 128), F32),
            pltpu.VMEM((8, 64, 128), F32),
            dma((32,)), dma((40,)), dma((16,)), dma((16,)), dma((32,)), dma((64,)), dma(()), dma((8,)),
            dma((16,)), dma((16,)), dma(()), dma(()), dma(()), dma((32,)), dma((8,)), dma((8,)), dma((4,)),
        ],
        compiler_params=pltpu.CompilerParams(
            collective_id=0, has_side_effects=True, vmem_limit_bytes=32 * 1024 * 1024
        ),
    )(features, queries, damping)


def split2(v):
    hi = v.astype(BF16)
    return hi, (v - hi.astype(F32)).astype(BF16)


def split3(v):
    hi = v.astype(BF16)
    rest = v - hi.astype(F32)
    mid = rest.astype(BF16)
    return hi, mid, (rest - mid.astype(F32)).astype(BF16)


def tn(a, b):
    return lax.dot_general(a, b, (((0,), (0,)), ((), ())), preferred_element_type=F32)


def nn(a, b):
    return lax.dot_general(a, b, (((1,), (0,)), ((), ())), preferred_element_type=F32)


def nt(a, b):
    return lax.dot_general(a, b, (((1,), (1,)), ((), ())), preferred_element_type=F32)


WIDTH = 32


def factor_kernel(fp, dp, out, mat):
    rows = lax.broadcasted_iota(jnp.int32, (PIV, PIV), 0)
    cols = lax.broadcasted_iota(jnp.int32, (PIV, PIV), 1)
    diag = jnp.concatenate([dp[0:1, :], dp[1:2, :]], axis=1)
    mat[...] = tn(fp[...], fp[...]) * (1.0 / SLAB) + jnp.where(rows == cols, diag, 0.0)

    row_w = lax.broadcasted_iota(jnp.int32, (WIDTH, 1), 0)
    lane_w = lax.broadcasted_iota(jnp.int32, (WIDTH, PIV), 1)
    aug_eye = jnp.where(
        lax.broadcasted_iota(jnp.int32, (WIDTH, 128), 0) == lax.broadcasted_iota(jnp.int32, (WIDTH, 128), 1),
        jnp.float32(1.0), jnp.float32(0.0),
    )

    @pl.loop(0, PIV // WIDTH)
    def _(k):
        c0 = pl.multiple_of(k * WIDTH, WIDTH)
        r = pltpu.roll(mat[pl.ds(c0, WIDTH), :], lax.rem(PIV - c0, PIV), 1)
        aug = aug_eye
        scale = jnp.zeros((WIDTH, 1), F32)
        for j0 in range(0, WIDTH, 8):
            column = [jnp.broadcast_to(r[:, j0 + t : j0 + t + 1], (WIDTH, 128)) for t in range(8)]
            for t in range(8):
                j = j0 + t
                pivot = column[t][j : j + 1, :]
                scale = scale + jnp.where(row_w == j, pivot[:, 0:1], 0.0)
                m = jnp.where(row_w > j, column[t] * (1.0 / pivot), 0.0)
                for u in range(t + 1, 8):
                    column[u] = column[u] - m * column[u][j : j + 1, :]
                r = r - jnp.concatenate([m, m], axis=1) * r[j : j + 1, :]
                aug = aug - m * aug[j : j + 1, :]
        s = lax.rsqrt(scale)
        s = s * (1.5 - 0.5 * scale * s * s)
        r = r * s
        aug = aug * s
        r = pltpu.roll(r, c0, 1)
        aug = pltpu.roll(jnp.concatenate([aug, jnp.zeros((WIDTH, 128), F32)], axis=1), c0, 1)
        inside = (lane_w >= c0) & (lane_w < c0 + WIDTH)
        v = jnp.where(inside, aug, r)
        mat[pl.ds(c0, WIDTH), :] = v
        below = jnp.where(lane_w >= c0 + WIDTH, r, 0.0)
        a1, a2, a3 = split3(below)
        b1, b2, b3 = split3(v)
        lhs = jnp.concatenate([a1, a1, a2, a1, a2, a3], axis=0)
        rhs = jnp.concatenate([b1, b2, b1, b3, b2, b1], axis=0)
        change = tn(lhs, rhs)
        old = mat[...]
        fresh = (cols >= c0) & (cols < c0 + WIDTH) & (rows >= c0 + WIDTH)
        mat[...] = jnp.where(fresh, 0.0, old) - change

    out[...] = jnp.where(rows >= cols, mat[...], 0.0)


def factor_inverse(fp, dp):
    vmem = pl.BlockSpec(memory_space=pltpu.VMEM)
    return pl.pallas_call(
        factor_kernel,
        name="factor",
        out_shape=jax.ShapeDtypeStruct((PIV, PIV), F32),
        in_specs=[vmem] * 2,
        out_specs=vmem,
        scratch_shapes=[pltpu.VMEM((PIV, PIV), F32)],
    )(fp, dp)


TILE = 512


def final_kernel(fj, fi, fp, linv, drow, sc, kout, fout, sout, fit, fpt, xcat, lcat):
    w = lax.axis_index("wide")
    z = lax.axis_index("narrow")
    t = pl.program_id(0)

    @pl.when(t == 0)
    def _():
        fit[...] = (fi[...] * jnp.asarray(1.0 / SLAB, BF16)).T
        fpt[...] = (fp[...] * jnp.asarray(1.0 / SLAB, BF16)).T
        l1, l2, l3 = split3(linv[...])
        lcat[:, 0:256] = l1
        lcat[:, 256:512] = l2
        lcat[:, 512:768] = l3
        a = nn(fit[...], fp[...])
        row = w * 512 + lax.broadcasted_iota(jnp.int32, (512, PIV), 0)
        col = lax.broadcasted_iota(jnp.int32, (512, PIV), 1)
        damp = jnp.broadcast_to(drow[...], (512, PIV))
        a = a + jnp.where(row == col, damp, 0.0)
        a1, a2, a3 = split3(a)
        xrow = (
            nt(a1, l1) + (nt(a1, l2) + nt(a2, l1)) + (nt(a1, l3) + nt(a2, l2) + nt(a3, l1))
        )
        xrow = jnp.where((row < 128) & (col >= 128), 0.0, xrow)
        fout[...] = xrow
        hi, lo = split2(xrow)
        xcat[:, 0:256] = -hi
        xcat[:, 256:512] = -hi
        xcat[:, 512:768] = -lo
        sout[...] = sc[...]

    b = nn(fpt[...], fj[...])
    b1, b2, b3 = split3(b)
    l1, l2, l3 = lcat[:, 0:256], lcat[:, 256:512], lcat[:, 512:768]
    xt = nn(l1, b1) + (nn(l1, b2) + nn(l2, b1))
    hi, lo = split2(xt)
    k = nn(fit[...], fj[...]) + nn(xcat[...], jnp.concatenate([hi, lo, hi], axis=0))
    row = w * 512 + lax.broadcasted_iota(jnp.int32, (512, TILE), 0)
    col = z * 2048 + t * TILE + lax.broadcasted_iota(jnp.int32, (512, TILE), 1)
    damp = jnp.broadcast_to(drow[...], (512, TILE))
    k = k + jnp.where(row == col, damp, 0.0)
    kout[...] = jnp.where((row < PIV) | (col < PIV), 0.0, k)


def finish(fj, fi, fp, linv, drow, sc):
    def whole(shape):
        return pl.BlockSpec(shape, lambda t: (0,) * len(shape))

    return pl.pallas_call(
        final_kernel,
        name="finish",
        grid=(2048 // TILE,),
        out_shape=[
            jax.ShapeDtypeStruct((512, 2048), F32),
            jax.ShapeDtypeStruct((512, PIV), F32),
            jax.ShapeDtypeStruct((64, 128), F32),
        ],
        in_specs=[
            pl.BlockSpec((SLAB, TILE), lambda t: (0, t)),
            whole((SLAB, 512)), whole((SLAB, PIV)), whole((PIV, PIV)), whole((512, 1)), whole((64, 128)),
        ],
        out_specs=[pl.BlockSpec((512, TILE), lambda t: (0, t)), whole((512, PIV)), whole((64, 128))],
        scratch_shapes=[
            pltpu.VMEM((512, SLAB), BF16),
            pltpu.VMEM((PIV, SLAB), BF16),
            pltpu.VMEM((512, 768), BF16),
            pltpu.VMEM((PIV, 768), BF16),
        ],
        compiler_params=pltpu.CompilerParams(vmem_limit_bytes=40 * 1024 * 1024),
    )(fj, fi, fp, linv, drow, sc)


def on_device(features, queries, damping):
    fj, fi, fp, dp, sc = gather(features, queries, damping.reshape(4, 128))
    linv = factor_inverse(fp, dp)
    return tuple(finish(fj, fi, fp, linv, damping.reshape(512, 1), sc))


def solution(mesh):
    return jax.shard_map(
        on_device,
        mesh=mesh,
        in_specs=(P("wide", "narrow"), P("wide", "narrow"), P("wide")),
        out_specs=(P("wide", "narrow"), P("wide", None), P("wide", "narrow")),
        check_vma=False,
    )
```

```python
import functools
import math

import jax
import jax.numpy as jnp
from jax import lax
from jax.experimental import pallas as pl
from jax.experimental.pallas import tpu as pltpu
from jax.sharding import PartitionSpec as P

P_SIZE = 16384
PIV = 256
SLAB = 1024
MESH = pl.DeviceIdType.MESH
F32 = jnp.float32
BF16 = jnp.bfloat16

ORDER = (
    (0, 0), (3, 0), (1, 0), (0, 3), (0, 1), (2, 0), (3, 3), (1, 3),
    (3, 1), (1, 1), (2, 3), (2, 1), (0, 2), (3, 2), (1, 2), (2, 2),
)
RELAYED = 10
LAST_STEP = 25


def _table(values, p):
    out = jnp.int32(0)
    for k, v in enumerate(values):
        if v:
            out = out + jnp.where(p == k, jnp.int32(v), jnp.int32(0))
    return out


def split2(v):
    hi = v.astype(BF16)
    return hi, (v - hi.astype(F32)).astype(BF16)


def split3(v):
    hi = v.astype(BF16)
    rest = v - hi.astype(F32)
    mid = rest.astype(BF16)
    return hi, mid, (rest - mid.astype(F32)).astype(BF16)


def tn(a, b):
    return lax.dot_general(a, b, (((0,), (0,)), ((), ())), preferred_element_type=F32)


def nn(a, b):
    return lax.dot_general(a, b, (((1,), (0,)), ((), ())), preferred_element_type=F32)


def nt(a, b):
    return lax.dot_general(a, b, (((1,), (1,)), ((), ())), preferred_element_type=F32)


WIDTH = 32
PANELS = PIV // WIDTH
TILE = 512


def panel_step(k, mat, rows, cols):
    row_w = lax.broadcasted_iota(jnp.int32, (WIDTH, 1), 0)
    lane_w = lax.broadcasted_iota(jnp.int32, (WIDTH, PIV), 1)
    aug = jnp.where(
        lax.broadcasted_iota(jnp.int32, (WIDTH, 128), 0) == lax.broadcasted_iota(jnp.int32, (WIDTH, 128), 1),
        jnp.float32(1.0), jnp.float32(0.0),
    )
    c0 = pl.multiple_of(k * WIDTH, WIDTH)
    r = pltpu.roll(mat[pl.ds(c0, WIDTH), :], lax.rem(PIV - c0, PIV), 1)
    scale = jnp.zeros((WIDTH, 1), F32)
    for j0 in range(0, WIDTH, 8):
        column = [jnp.broadcast_to(r[:, j0 + t : j0 + t + 1], (WIDTH, 128)) for t in range(8)]
        for t in range(8):
            j = j0 + t
            pivot = column[t][j : j + 1, :]
            scale = scale + jnp.where(row_w == j, pivot[:, 0:1], 0.0)
            m = jnp.where(row_w > j, column[t] * (1.0 / pivot), 0.0)
            for u in range(t + 1, 8):
                column[u] = column[u] - m * column[u][j : j + 1, :]
            r = r - jnp.concatenate([m, m], axis=1) * r[j : j + 1, :]
            aug = aug - m * aug[j : j + 1, :]
    s = lax.rsqrt(scale)
    s = s * (1.5 - 0.5 * scale * s * s)
    r = r * s
    aug = aug * s
    r = pltpu.roll(r, c0, 1)
    aug = pltpu.roll(jnp.concatenate([aug, jnp.zeros((WIDTH, 128), F32)], axis=1), c0, 1)
    inside = (lane_w >= c0) & (lane_w < c0 + WIDTH)
    v = jnp.where(inside, aug, r)
    mat[pl.ds(c0, WIDTH), :] = v
    below = jnp.where(lane_w >= c0 + WIDTH, r, 0.0)
    a1, a2, a3 = split3(below)
    b1, b2, b3 = split3(v)
    lhs = jnp.concatenate([a1, a1, a2, a1, a2, a3], axis=0)
    rhs = jnp.concatenate([b1, b2, b1, b3, b2, b1], axis=0)
    change = tn(lhs, rhs)
    fresh = (cols >= c0) & (cols < c0 + WIDTH) & (rows >= c0 + WIDTH)
    mat[...] = jnp.where(fresh, 0.0, mat[...]) - change


def gather_kernel(
    feat, qry_hbm, damp, fj, fi, fp, linv, xhi, xlo, sc,
    qry, dp, fpt, mat, part, inbox,
    ag_recv, ag_send, pt_recv, pt_send, z_recv, z_send, fpz_recv, fpz_send,
    fp_recv, fp_send, fpp_recv, fpp_send, d_recv, d_send, rs_recv, rs_send, local,
):
    w = lax.axis_index("wide")
    z = lax.axis_index("narrow")
    c = lax.rem(w, 2)
    x = lax.rem(lax.div(w, 2), 4)
    y = lax.div(w, 8)

    def spot(da, db, core):
        px = lax.rem(x + da + core * (db - da), 4)
        py = lax.rem(y + db + core * (da - db), 4)
        return px, py

    def dev(da, db):
        px, py = spot(da, db, c)
        return ((py * 4 + px) * 2 + c, z)

    def row(da, db, core):
        px, py = spot(da, db, core)
        return pl.multiple_of((core * 16 + py * 4 + px) * 32, 32)

    partner = (w + 1 - 2 * c, z)
    own = row(0, 0, c)

    def rcopy(src, dst, ssem, rsem, to):
        return pltpu.make_async_remote_copy(
            src_ref=src, dst_ref=dst, send_sem=ssem, recv_sem=rsem, device_id=to, device_id_type=MESH
        )

    fj_own = pltpu.make_async_copy(feat, fj.at[pl.ds(own, 32), :], local.at[1])
    fj_own.start()
    qry_copy = pltpu.make_async_copy(qry_hbm, qry, local.at[2])
    qry_copy.start()
    dp_own = pltpu.make_async_copy(damp, dp, local.at[4])

    @pl.when(w == 0)
    def _():
        dp_own.start()

    barrier = pltpu.get_barrier_semaphore()

    @pl.loop(1, 16)
    def _(k):
        pl.semaphore_signal(
            barrier, inc=1, device_id=dev(lax.div(k, 4), lax.rem(k, 4)), device_id_type=MESH
        )

    @pl.loop(1, 8)
    def _(k):
        pl.semaphore_signal(barrier, inc=1, device_id=(w, lax.rem(z + k, 8)), device_id_type=MESH)

    pl.semaphore_signal(barrier, inc=1, device_id=partner, device_id_type=MESH)
    fj_own.wait()
    pl.semaphore_wait(barrier, 23)

    def fpz(k):
        return rcopy(
            fj.at[pl.ds(own, 32), pl.ds(0, PIV)], fp.at[pl.ds(own, 32), :], fpz_send.at[k], fpz_recv,
            (w, lax.rem(z + k, 8)),
        )

    fp_own = pltpu.make_async_copy(
        fj.at[pl.ds(own, 32), pl.ds(0, PIV)], fp.at[pl.ds(own, 32), :], local.at[0]
    )

    def dcopy(k):
        return rcopy(dp, dp, d_send.at[k], d_recv, dev(lax.div(k, 4), lax.rem(k, 4)))

    d_across = rcopy(dp, dp, d_send.at[16], d_recv, partner)

    @pl.when(z == 0)
    def _():
        for k in (4, 3, 5, 2, 6, 1, 7):
            fpz(k).start()
        fp_own.start()

    @pl.when(w == 0)
    def _():
        dp_own.wait()

        @pl.loop(1, 16)
        def _(k):
            dcopy(k).start()


    sends = []

    def send_block(da, db, half, to, as_da, as_db):
        n = len(sends)
        r = row(da, db, c)
        if half is None:
            rows, index = pl.ds(r, 32), (as_da * 4 + as_db) * 2
        else:
            rows, index = pl.ds(r + 16 * half, 16), (as_da * 4 + as_db) * 2 + half
        op = rcopy(
            fj.at[rows, :], fj.at[rows, :],
            ag_send.at[n], ag_recv.at[index], to,
        )
        op.start()
        sends.append(op)

    def wait_block(da, db):
        r = row(da, db, c)
        base = (da * 4 + db) * 2
        if da == 2 and db == 0 or db == 2:
            for h in range(2):
                ref = fj.at[pl.ds(r + 16 * h, 16), :]
                rcopy(ref, ref, ag_send.at[0], ag_recv.at[base + h], partner).wait_recv()
        else:
            ref = fj.at[pl.ds(r, 32), :]
            rcopy(ref, ref, ag_send.at[0], ag_recv.at[base], partner).wait_recv()

    def to_partner(p):
        da, db = ORDER[p]
        ref = fj.at[pl.ds(row(da, db, c), 32), :]
        op = rcopy(ref, ref, pt_send.at[p], pt_recv.at[p], partner)
        op.start()
        sends.append(op)

    def plane_event(p):
        da, db = ORDER[p]
        if p:
            wait_block(da, db)
        if db == 0:
            if da == 0:
                send_block(0, 0, None, dev(1, 0), 3, 0)
                send_block(0, 0, None, dev(3, 0), 1, 0)
            elif da == 3:
                send_block(3, 0, 0, dev(1, 0), 2, 0)
            elif da == 1:
                send_block(1, 0, 1, dev(3, 0), 2, 0)
            send_block(da, 0, None, dev(0, 1), da, 3)
            send_block(da, 0, None, dev(0, 3), da, 1)
        elif db == 3:
            send_block(da, 3, 0, dev(0, 1), da, 2)
        elif db == 1:
            send_block(da, 1, 1, dev(0, 3), da, 2)
        to_partner(p)

    def fp_direct(k):
        da, db = lax.div(k, 4), lax.rem(k, 4)
        back = lax.rem(4 - da, 4) * 4 + lax.rem(4 - db, 4)
        ref = fp.at[pl.ds(own, 32), :]
        return rcopy(ref, ref, fp_send.at[k], fp_recv.at[back], dev(da, db))

    half_rows = fp.at[pl.ds(pl.multiple_of(c * 512, 512), 512), :]
    fp_half = rcopy(half_rows, half_rows, fpp_send, fpp_recv, partner)

    def panel_start():
        @pl.when(z == 0)
        def _():
            fp_own.wait()

        @pl.when(z != 0)
        def _():
            fpz(0).wait_recv()

        @pl.loop(1, 16)
        def _(k):
            fp_direct(k).start()

    def panel_to_partner():
        @pl.loop(1, 16)
        def _(k):
            fp_direct(k).wait_recv()

        fp_half.start()

        @pl.when(c == 0)
        def _():
            @pl.when(w != 0)
            def _():
                dcopy(0).wait_recv()

            d_across.start()

    home = lax.div(w, 4)
    d = lax.rem(z - home + 8, 8)
    sub = pl.multiple_of(lax.rem(w, 4) * 512, 512)
    up = (w, lax.rem(z + 1, 8))
    down = (w, lax.rem(z + 7, 8))
    hops_up = d
    hops_down = lax.rem(8 - d, 8)
    near = jnp.minimum(hops_up, hops_down)

    def z_rows(p, s):
        da = _table([o[0] for o in ORDER], p)
        db = _table([o[1] for o in ORDER], p)
        core = c if s == 0 else 1 - c
        return row(da, db, core)

    def z_copy(p, s, from_root, to, way):
        r = z_rows(p, s)
        dst = fi.at[pl.ds(r, 32), :]
        src = fj.at[pl.ds(r, 32), pl.ds(sub, 512)] if from_root else dst
        q = p * 2 + s
        return rcopy(src, dst, z_send.at[q * 2 + way], z_recv.at[q], to)

    def pt_wait(p):
        ref = fj.at[pl.ds(z_rows(p, 1), 32), :]
        rcopy(ref, ref, pt_send.at[0], pt_recv.at[p], partner).wait_recv()

    def z_step(t):
        first = t - 1

        @pl.when((d == 0) & (first >= 0) & (first < RELAYED))
        def _():
            z_copy(first, 0, True, up, 0).start()
            pt_wait(first)
            z_copy(first, 1, True, down, 1).start()

        @pl.when((d == 0) & (first >= RELAYED) & (first < 16))
        def _():
            z_copy(first, 0, True, up, 0).start()
            z_copy(first, 0, True, down, 1).start()
            pt_wait(first)
            z_copy(first, 1, True, up, 0).start()
            z_copy(first, 1, True, down, 1).start()

        pu = first - 2 * hops_up

        @pl.when((d != 0) & (pu >= 0) & (pu < RELAYED))
        def _():
            z_copy(pu, 0, False, up, 0).wait_recv()

            @pl.when(d < 7)
            def _():
                z_copy(pu, 0, False, up, 0).start()

        pd = first - 2 * hops_down

        @pl.when((d != 0) & (pd >= 0) & (pd < RELAYED))
        def _():
            z_copy(pd, 1, False, down, 1).wait_recv()

            @pl.when(d > 1)
            def _():
                z_copy(pd, 1, False, down, 1).start()

        pn = first - 2 * near

        @pl.when((d != 0) & (pn >= RELAYED) & (pn < 16))
        def _():
            for s in range(2):
                z_copy(pn, s, False, up, 0).wait_recv()

                @pl.when(d < 4)
                def _():
                    z_copy(pn, s, False, up, 0).start()

                @pl.when(d > 5)
                def _():
                    z_copy(pn, s, False, down, 1).start()

    def plane_tail(p):
        r = z_rows(p, 0)
        da = _table([o[0] for o in ORDER], p)
        for h in range(2):
            ref = fj.at[pl.ds(r + 16 * h, 16), :]
            rcopy(ref, ref, ag_send.at[0], ag_recv.at[(da * 4 + 2) * 2 + h], partner).wait_recv()
        ref = fj.at[pl.ds(r, 32), :]
        rcopy(ref, ref, pt_send.at[p], pt_recv.at[p], partner).start()

    fi_own = pltpu.make_async_copy(fj.at[:, pl.ds(sub, 512)], fi, local.at[3])

    def scores_for(k):
        yk = lax.div(k, 2)
        xk = lax.rem(k, 2) * 2
        pieces = []
        for dx in range(2):
            for core in range(2):
                r = pl.multiple_of((core * 16 + yk * 4 + xk + dx) * 32, 32)
                pieces.append(fj[pl.ds(r, 32), :])
        return lax.dot_general(
            qry[...], jnp.concatenate(pieces, axis=0), (((1,), (1,)), ((), ())),
            preferred_element_type=F32,
        )

    def rs_copy(k):
        to = lax.rem(z + k, 8)
        return rcopy(part.at[to], inbox.at[k], rs_send.at[k], rs_recv.at[k], (w, to))

    def plane_done():
        @pl.when(d != 0)
        def _():
            @pl.loop(0, 16)
            def _(p):
                pt_wait(p)

        @pl.when(d == 0)
        def _():
            fi_own.start()

        qry_copy.wait()

        @pl.loop(1, 8)
        def _(k):
            part[lax.rem(z + k, 8)] = scores_for(lax.rem(z + k, 8))
            rs_copy(k).start()

        part[z] = scores_for(z)

    for t in range(12):
        plane_event(t)
        if t == 4:
            panel_start()
        if t == 9:
            panel_to_partner()
        z_step(jnp.int32(t))

    fp_half.wait_recv()

    @pl.when(c != 0)
    def _():
        d_across.wait_recv()

    rows = lax.broadcasted_iota(jnp.int32, (PIV, PIV), 0)
    cols = lax.broadcasted_iota(jnp.int32, (PIV, PIV), 1)
    diag = jnp.concatenate([dp[0:1, :], dp[1:2, :]], axis=1)
    fpt[...] = (fp[...] * jnp.asarray(1.0 / SLAB, BF16)).T
    mat[...] = nn(fpt[...], fp[...]) + jnp.where(rows == cols, diag, 0.0)

    @pl.loop(0, PANELS)
    def _(k):
        @pl.when(k < 4)
        def _():
            plane_tail(12 + k)

        z_step(12 + k)

        @pl.when(k == 4)
        def _():
            plane_done()

        panel_step(k, mat, rows, cols)

    linv[...] = jnp.where(rows >= cols, mat[...], 0.0)

    @pl.loop(0, 2048 // TILE)
    def _(t):
        z_step(12 + PANELS + t)
        lanes = pl.ds(pl.multiple_of(t * TILE, TILE), TILE)
        b1, b2, _b = split3(nn(fpt[...], fj[:, lanes]))
        l1, l2, _l = split3(linv[...])
        hi, lo = split2(nn(l1, b1) + (nn(l1, b2) + nn(l2, b1)))
        xhi[:, lanes] = hi
        xlo[:, lanes] = lo

    @pl.loop(12 + PANELS + 2048 // TILE, LAST_STEP)
    def _(t):
        z_step(t)

    total = part[z]
    for k in range(1, 8):
        rs_copy(k).wait_recv()
        total = total + inbox[k]
    sc[...] = total * (1.0 / math.sqrt(P_SIZE))

    @pl.when(d == 0)
    def _():
        fi_own.wait()

    fp_half.wait_send()

    @pl.when(w == 0)
    def _():
        @pl.loop(1, 16)
        def _(k):
            dcopy(k).wait_send()

    @pl.when(c == 0)
    def _():
        d_across.wait_send()

    @pl.when(z == 0)
    def _():
        for k in range(1, 8):
            fpz(k).wait_send()

    @pl.loop(1, 16)
    def _(k):
        fp_direct(k).wait_send()

    @pl.loop(1, 8)
    def _(k):
        rs_copy(k).wait_send()

    for op in sends:
        op.wait_send()

    @pl.loop(12, 16)
    def _(p):
        ref = fj.at[pl.ds(z_rows(p, 0), 32), :]
        rcopy(ref, ref, pt_send.at[p], pt_recv.at[p], partner).wait_send()

    @pl.loop(0, 16)
    def _(p):
        one_way = p < RELAYED

        @pl.when(one_way & (d < 7))
        def _():
            z_copy(p, 0, False, up, 0).wait_send()

        @pl.when(one_way & (d != 1))
        def _():
            z_copy(p, 1, False, down, 1).wait_send()

        for s in range(2):
            @pl.when(jnp.logical_not(one_way) & (d < 4))
            def _():
                z_copy(p, s, False, up, 0).wait_send()

            @pl.when(jnp.logical_not(one_way) & ((d > 5) | (d == 0)))
            def _():
                z_copy(p, s, False, down, 1).wait_send()


def gather(features, queries, damping):
    vmem = pl.BlockSpec(memory_space=pltpu.VMEM)
    hbm = pl.BlockSpec(memory_space=pltpu.HBM)
    dma = pltpu.SemaphoreType.DMA
    return pl.pallas_call(
        gather_kernel,
        name="gather",
        out_shape=[
            jax.ShapeDtypeStruct((SLAB, 2048), BF16),
            jax.ShapeDtypeStruct((SLAB, 512), BF16),
            jax.ShapeDtypeStruct((SLAB, PIV), BF16),
            jax.ShapeDtypeStruct((PIV, PIV), F32),
            jax.ShapeDtypeStruct((PIV, 2048), BF16),
            jax.ShapeDtypeStruct((PIV, 2048), BF16),
            jax.ShapeDtypeStruct((64, 128), F32),
        ],
        in_specs=[hbm] * 3,
        out_specs=[vmem] * 7,
        scratch_shapes=[
            pltpu.VMEM((64, 2048), BF16),
            pltpu.VMEM((4, 128), F32),
            pltpu.VMEM((PIV, SLAB), BF16),
            pltpu.VMEM((PIV, PIV), F32),
            pltpu.VMEM((8, 64, 128), F32),
            pltpu.VMEM((8, 64, 128), F32),
            dma((32,)), dma((40,)), dma((16,)), dma((16,)), dma((32,)), dma((64,)), dma(()), dma((8,)),
            dma((16,)), dma((16,)), dma(()), dma(()), dma(()), dma((17,)), dma((8,)), dma((8,)), dma((5,)),
        ],
        compiler_params=pltpu.CompilerParams(
            collective_id=0, has_side_effects=True, vmem_limit_bytes=40 * 1024 * 1024
        ),
    )(features, queries, damping)


def final_kernel(fj, xhi, xlo, fi, fp, linv, damp, sc, kout, fout, sout, fit, xcat):
    w = lax.axis_index("wide")
    z = lax.axis_index("narrow")
    t = pl.program_id(0)

    @pl.when(t == 0)
    def _():
        fit[...] = (fi[...] * jnp.asarray(1.0 / SLAB, BF16)).T
        a = nn(fit[...], fp[...])
        row = w * 512 + lax.broadcasted_iota(jnp.int32, (512, PIV), 0)
        col = lax.broadcasted_iota(jnp.int32, (512, PIV), 1)
        lanes = jnp.concatenate([damp[0:1, :], damp[1:2, :]], axis=1)
        a = a + jnp.where(row == col, lanes, 0.0)
        a1, a2, a3 = split3(a)
        l1, l2, l3 = split3(linv[...])
        xrow = (
            nt(a1, l1) + (nt(a1, l2) + nt(a2, l1)) + (nt(a1, l3) + nt(a2, l2) + nt(a3, l1))
        )
        xrow = jnp.where((row < 128) & (col >= 128), 0.0, xrow)
        fout[...] = xrow
        hi, lo = split2(xrow)
        xcat[:, 0:256] = -hi
        xcat[:, 256:512] = -hi
        xcat[:, 512:768] = -lo
        sout[...] = sc[...]

    k = nn(fit[...], fj[...]) + nn(xcat[...], jnp.concatenate([xhi[...], xlo[...], xhi[...]], axis=0))
    row = lax.broadcasted_iota(jnp.int32, (512, TILE), 0)
    lane = lax.broadcasted_iota(jnp.int32, (512, TILE), 1)
    col = z * 2048 + t * TILE
    lanes = jnp.concatenate([damp[i : i + 1, :] for i in range(4)], axis=1)
    k = k + jnp.where((row == lane) & (col == w * 512), lanes, 0.0)
    kout[...] = jnp.where((w * 512 + row < PIV) | (col + lane < PIV), 0.0, k)


def finish(fj, fi, fp, linv, xhi, xlo, sc, damping):
    def whole(shape):
        return pl.BlockSpec(shape, lambda t: (0,) * len(shape))

    def tiled(rows):
        return pl.BlockSpec((rows, TILE), lambda t: (0, t))

    return pl.pallas_call(
        final_kernel,
        name="finish",
        grid=(2048 // TILE,),
        out_shape=[
            jax.ShapeDtypeStruct((512, 2048), F32),
            jax.ShapeDtypeStruct((512, PIV), F32),
            jax.ShapeDtypeStruct((64, 128), F32),
        ],
        in_specs=[
            tiled(SLAB), tiled(PIV), tiled(PIV),
            whole((SLAB, 512)), whole((SLAB, PIV)), whole((PIV, PIV)), whole((4, 128)), whole((64, 128)),
        ],
        out_specs=[tiled(512), whole((512, PIV)), whole((64, 128))],
        scratch_shapes=[
            pltpu.VMEM((512, SLAB), BF16),
            pltpu.VMEM((512, 768), BF16),
        ],
        compiler_params=pltpu.CompilerParams(vmem_limit_bytes=40 * 1024 * 1024),
    )(fj, xhi, xlo, fi, fp, linv, damping, sc)


def on_device(features, queries, damping):
    damping = damping.reshape(4, 128)
    return tuple(finish(*gather(features, queries, damping), damping))


def solution(mesh):
    return jax.shard_map(
        on_device,
        mesh=mesh,
        in_specs=(P("wide", "narrow"), P("wide", "narrow"), P("wide")),
        out_specs=(P("wide", "narrow"), P("wide", None), P("wide", "narrow")),
        check_vma=False,
    )
```

```python
import functools
import math

import jax
import jax.numpy as jnp
from jax import lax
from jax.experimental import pallas as pl
from jax.experimental.pallas import tpu as pltpu
from jax.sharding import PartitionSpec as P

P_SIZE = 16384
PIV = 256
SLAB = 1024
MESH = pl.DeviceIdType.MESH
F32 = jnp.float32
BF16 = jnp.bfloat16

ORDER = (
    (0, 0), (3, 0), (1, 0), (0, 3), (0, 1), (2, 0), (3, 3), (1, 3),
    (3, 1), (1, 1), (2, 3), (2, 1), (0, 2), (3, 2), (1, 2), (2, 2),
)
RELAYED = 6
LAG = 3
LAST_STEP = max(RELAYED + 7 * LAG if RELAYED else 0, 16 + 4 * LAG) + 1


def _table(values, p):
    out = jnp.int32(0)
    for k, v in enumerate(values):
        if v:
            out = out + jnp.where(p == k, jnp.int32(v), jnp.int32(0))
    return out


def split2(v):
    hi = v.astype(BF16)
    return hi, (v - hi.astype(F32)).astype(BF16)


def split3(v):
    hi = v.astype(BF16)
    rest = v - hi.astype(F32)
    mid = rest.astype(BF16)
    return hi, mid, (rest - mid.astype(F32)).astype(BF16)


def tn(a, b):
    return lax.dot_general(a, b, (((0,), (0,)), ((), ())), preferred_element_type=F32)


def nn(a, b):
    return lax.dot_general(a, b, (((1,), (0,)), ((), ())), preferred_element_type=F32)


def nt(a, b):
    return lax.dot_general(a, b, (((1,), (1,)), ((), ())), preferred_element_type=F32)


WIDTH = 32
PANELS = PIV // WIDTH
TILE = 512


def panel_step(k, mat, rows, cols):
    row_w = lax.broadcasted_iota(jnp.int32, (WIDTH, 1), 0)
    lane_w = lax.broadcasted_iota(jnp.int32, (WIDTH, PIV), 1)
    aug = jnp.where(
        lax.broadcasted_iota(jnp.int32, (WIDTH, 128), 0) == lax.broadcasted_iota(jnp.int32, (WIDTH, 128), 1),
        jnp.float32(1.0), jnp.float32(0.0),
    )
    c0 = pl.multiple_of(k * WIDTH, WIDTH)
    r = pltpu.roll(mat[pl.ds(c0, WIDTH), :], lax.rem(PIV - c0, PIV), 1)
    scale = jnp.zeros((WIDTH, 1), F32)
    for j0 in range(0, WIDTH, 8):
        column = [jnp.broadcast_to(r[:, j0 + t : j0 + t + 1], (WIDTH, 128)) for t in range(8)]
        for t in range(8):
            j = j0 + t
            pivot = column[t][j : j + 1, :]
            scale = scale + jnp.where(row_w == j, pivot[:, 0:1], 0.0)
            m = jnp.where(row_w > j, column[t] * (1.0 / pivot), 0.0)
            for u in range(t + 1, 8):
                column[u] = column[u] - m * column[u][j : j + 1, :]
            r = r - jnp.concatenate([m, m], axis=1) * r[j : j + 1, :]
            aug = aug - m * aug[j : j + 1, :]
    s = lax.rsqrt(scale)
    s = s * (1.5 - 0.5 * scale * s * s)
    r = r * s
    aug = aug * s
    r = pltpu.roll(r, c0, 1)
    aug = pltpu.roll(jnp.concatenate([aug, jnp.zeros((WIDTH, 128), F32)], axis=1), c0, 1)
    inside = (lane_w >= c0) & (lane_w < c0 + WIDTH)
    v = jnp.where(inside, aug, r)
    mat[pl.ds(c0, WIDTH), :] = v
    below = jnp.where(lane_w >= c0 + WIDTH, r, 0.0)
    a1, a2, a3 = split3(below)
    b1, b2, b3 = split3(v)
    lhs = jnp.concatenate([a1, a1, a2, a1, a2, a3], axis=0)
    rhs = jnp.concatenate([b1, b2, b1, b3, b2, b1], axis=0)
    change = tn(lhs, rhs)
    fresh = (cols >= c0) & (cols < c0 + WIDTH) & (rows >= c0 + WIDTH)
    mat[...] = jnp.where(fresh, 0.0, mat[...]) - change


def gather_kernel(
    feat, qry_hbm, damp, fj, fi, fp, linv, xhi, xlo, sc,
    qry, dp, fpt, mat, part, inbox,
    ag_recv, ag_send, pt_recv, pt_send, z_recv, z_send, fpz_recv, fpz_send,
    fp_recv, fp_send, fpp_recv, fpp_send, d_recv, d_send, rs_recv, rs_send, local,
):
    w = lax.axis_index("wide")
    z = lax.axis_index("narrow")
    c = lax.rem(w, 2)
    x = lax.rem(lax.div(w, 2), 4)
    y = lax.div(w, 8)

    def spot(da, db, core):
        px = lax.rem(x + da + core * (db - da), 4)
        py = lax.rem(y + db + core * (da - db), 4)
        return px, py

    def dev(da, db):
        px, py = spot(da, db, c)
        return ((py * 4 + px) * 2 + c, z)

    def row(da, db, core):
        px, py = spot(da, db, core)
        return pl.multiple_of((core * 16 + py * 4 + px) * 32, 32)

    partner = (w + 1 - 2 * c, z)
    own = row(0, 0, c)

    def rcopy(src, dst, ssem, rsem, to):
        return pltpu.make_async_remote_copy(
            src_ref=src, dst_ref=dst, send_sem=ssem, recv_sem=rsem, device_id=to, device_id_type=MESH
        )

    fj_own = pltpu.make_async_copy(feat, fj.at[pl.ds(own, 32), :], local.at[1])
    fj_own.start()
    qry_copy = pltpu.make_async_copy(qry_hbm, qry, local.at[2])
    qry_copy.start()
    dp_own = pltpu.make_async_copy(damp, dp, local.at[4])

    @pl.when(w == 0)
    def _():
        dp_own.start()

    barrier = pltpu.get_barrier_semaphore()

    @pl.loop(1, 16)
    def _(k):
        pl.semaphore_signal(
            barrier, inc=1, device_id=dev(lax.div(k, 4), lax.rem(k, 4)), device_id_type=MESH
        )

    @pl.loop(1, 8)
    def _(k):
        pl.semaphore_signal(barrier, inc=1, device_id=(w, lax.rem(z + k, 8)), device_id_type=MESH)

    pl.semaphore_signal(barrier, inc=1, device_id=partner, device_id_type=MESH)
    fj_own.wait()
    pl.semaphore_wait(barrier, 23)

    def fpz(k):
        return rcopy(
            fj.at[pl.ds(own, 32), pl.ds(0, PIV)], fp.at[pl.ds(own, 32), :], fpz_send.at[k], fpz_recv,
            (w, lax.rem(z + k, 8)),
        )

    fp_own = pltpu.make_async_copy(
        fj.at[pl.ds(own, 32), pl.ds(0, PIV)], fp.at[pl.ds(own, 32), :], local.at[0]
    )

    def dcopy(k):
        return rcopy(dp, dp, d_send.at[k], d_recv, dev(lax.div(k, 4), lax.rem(k, 4)))

    d_across = rcopy(dp, dp, d_send.at[16], d_recv, partner)

    @pl.when(z == 0)
    def _():
        for k in (4, 3, 5, 2, 6, 1, 7):
            fpz(k).start()
        fp_own.start()

    @pl.when(w == 0)
    def _():
        dp_own.wait()

        @pl.loop(1, 16)
        def _(k):
            dcopy(k).start()


    sends = []

    def send_block(da, db, half, to, as_da, as_db):
        n = len(sends)
        r = row(da, db, c)
        if half is None:
            rows, index = pl.ds(r, 32), (as_da * 4 + as_db) * 2
        else:
            rows, index = pl.ds(r + 16 * half, 16), (as_da * 4 + as_db) * 2 + half
        op = rcopy(
            fj.at[rows, :], fj.at[rows, :],
            ag_send.at[n], ag_recv.at[index], to,
        )
        op.start()
        sends.append(op)

    def wait_block(da, db):
        r = row(da, db, c)
        base = (da * 4 + db) * 2
        if da == 2 and db == 0 or db == 2:
            for h in range(2):
                ref = fj.at[pl.ds(r + 16 * h, 16), :]
                rcopy(ref, ref, ag_send.at[0], ag_recv.at[base + h], partner).wait_recv()
        else:
            ref = fj.at[pl.ds(r, 32), :]
            rcopy(ref, ref, ag_send.at[0], ag_recv.at[base], partner).wait_recv()

    def to_partner(p):
        da, db = ORDER[p]
        ref = fj.at[pl.ds(row(da, db, c), 32), :]
        op = rcopy(ref, ref, pt_send.at[p], pt_recv.at[p], partner)
        op.start()
        sends.append(op)

    def plane_event(p):
        da, db = ORDER[p]
        if p:
            wait_block(da, db)
        if db == 0:
            if da == 0:
                send_block(0, 0, None, dev(1, 0), 3, 0)
                send_block(0, 0, None, dev(3, 0), 1, 0)
            elif da == 3:
                send_block(3, 0, 0, dev(1, 0), 2, 0)
            elif da == 1:
                send_block(1, 0, 1, dev(3, 0), 2, 0)
            send_block(da, 0, None, dev(0, 1), da, 3)
            send_block(da, 0, None, dev(0, 3), da, 1)
        elif db == 3:
            send_block(da, 3, 0, dev(0, 1), da, 2)
        elif db == 1:
            send_block(da, 1, 1, dev(0, 3), da, 2)
        to_partner(p)

    def fp_direct(k):
        da, db = lax.div(k, 4), lax.rem(k, 4)
        back = lax.rem(4 - da, 4) * 4 + lax.rem(4 - db, 4)
        ref = fp.at[pl.ds(own, 32), :]
        return rcopy(ref, ref, fp_send.at[k], fp_recv.at[back], dev(da, db))

    half_rows = fp.at[pl.ds(pl.multiple_of(c * 512, 512), 512), :]
    fp_half = rcopy(half_rows, half_rows, fpp_send, fpp_recv, partner)

    def panel_start():
        @pl.when(z == 0)
        def _():
            fp_own.wait()

        @pl.when(z != 0)
        def _():
            fpz(0).wait_recv()

        @pl.loop(1, 16)
        def _(k):
            fp_direct(k).start()

    def panel_to_partner():
        @pl.loop(1, 16)
        def _(k):
            fp_direct(k).wait_recv()

        fp_half.start()

        @pl.when(c == 0)
        def _():
            @pl.when(w != 0)
            def _():
                dcopy(0).wait_recv()

            d_across.start()

    home = lax.div(w, 4)
    d = lax.rem(z - home + 8, 8)
    sub = pl.multiple_of(lax.rem(w, 4) * 512, 512)
    up = (w, lax.rem(z + 1, 8))
    down = (w, lax.rem(z + 7, 8))
    hops_up = d
    hops_down = lax.rem(8 - d, 8)
    near = jnp.minimum(hops_up, hops_down)

    def z_rows(p, s):
        da = _table([o[0] for o in ORDER], p)
        db = _table([o[1] for o in ORDER], p)
        core = c if s == 0 else 1 - c
        return row(da, db, core)

    def z_copy(p, s, from_root, to, way):
        r = z_rows(p, s)
        dst = fi.at[pl.ds(r, 32), :]
        src = fj.at[pl.ds(r, 32), pl.ds(sub, 512)] if from_root else dst
        q = p * 2 + s
        return rcopy(src, dst, z_send.at[q * 2 + way], z_recv.at[q], to)

    def pt_wait(p):
        ref = fj.at[pl.ds(z_rows(p, 1), 32), :]
        rcopy(ref, ref, pt_send.at[0], pt_recv.at[p], partner).wait_recv()

    def z_step(t):
        first = t - 1

        @pl.when((d == 0) & (first >= 0) & (first < RELAYED))
        def _():
            z_copy(first, 0, True, up, 0).start()
            pt_wait(first)
            z_copy(first, 1, True, down, 1).start()

        @pl.when((d == 0) & (first >= RELAYED) & (first < 16))
        def _():
            z_copy(first, 0, True, up, 0).start()
            z_copy(first, 0, True, down, 1).start()
            pt_wait(first)
            z_copy(first, 1, True, up, 0).start()
            z_copy(first, 1, True, down, 1).start()

        pu = first - LAG * hops_up

        @pl.when((d != 0) & (pu >= 0) & (pu < RELAYED))
        def _():
            z_copy(pu, 0, False, up, 0).wait_recv()

            @pl.when(d < 7)
            def _():
                z_copy(pu, 0, False, up, 0).start()

        pd = first - LAG * hops_down

        @pl.when((d != 0) & (pd >= 0) & (pd < RELAYED))
        def _():
            z_copy(pd, 1, False, down, 1).wait_recv()

            @pl.when(d > 1)
            def _():
                z_copy(pd, 1, False, down, 1).start()

        pn = first - LAG * near

        @pl.when((d != 0) & (pn >= RELAYED) & (pn < 16))
        def _():
            for s in range(2):
                z_copy(pn, s, False, up, 0).wait_recv()

                @pl.when(d < 4)
                def _():
                    z_copy(pn, s, False, up, 0).start()

                @pl.when(d > 5)
                def _():
                    z_copy(pn, s, False, down, 1).start()

    def plane_tail(p):
        r = z_rows(p, 0)
        da = _table([o[0] for o in ORDER], p)
        for h in range(2):
            ref = fj.at[pl.ds(r + 16 * h, 16), :]
            rcopy(ref, ref, ag_send.at[0], ag_recv.at[(da * 4 + 2) * 2 + h], partner).wait_recv()
        ref = fj.at[pl.ds(r, 32), :]
        rcopy(ref, ref, pt_send.at[p], pt_recv.at[p], partner).start()

    fi_own = pltpu.make_async_copy(fj.at[:, pl.ds(sub, 512)], fi, local.at[3])

    def scores_for(k):
        yk = lax.div(k, 2)
        xk = lax.rem(k, 2) * 2
        pieces = []
        for dx in range(2):
            for core in range(2):
                r = pl.multiple_of((core * 16 + yk * 4 + xk + dx) * 32, 32)
                pieces.append(fj[pl.ds(r, 32), :])
        return lax.dot_general(
            qry[...], jnp.concatenate(pieces, axis=0), (((1,), (1,)), ((), ())),
            preferred_element_type=F32,
        )

    def rs_copy(k):
        to = lax.rem(z + k, 8)
        return rcopy(part.at[to], inbox.at[k], rs_send.at[k], rs_recv.at[k], (w, to))

    def plane_done():
        @pl.when(d != 0)
        def _():
            @pl.loop(0, 16)
            def _(p):
                pt_wait(p)

        @pl.when(d == 0)
        def _():
            fi_own.start()

        qry_copy.wait()

        @pl.loop(1, 8)
        def _(k):
            part[lax.rem(z + k, 8)] = scores_for(lax.rem(z + k, 8))
            rs_copy(k).start()

        part[z] = scores_for(z)

    for t in range(12):
        plane_event(t)
        if t == 4:
            panel_start()
        if t == 9:
            panel_to_partner()
        z_step(jnp.int32(t))

    fp_half.wait_recv()

    @pl.when(c != 0)
    def _():
        d_across.wait_recv()

    rows = lax.broadcasted_iota(jnp.int32, (PIV, PIV), 0)
    cols = lax.broadcasted_iota(jnp.int32, (PIV, PIV), 1)
    diag = jnp.concatenate([dp[0:1, :], dp[1:2, :]], axis=1)
    fpt[...] = (fp[...] * jnp.asarray(1.0 / SLAB, BF16)).T
    mat[...] = nn(fpt[...], fp[...]) + jnp.where(rows == cols, diag, 0.0)

    @pl.loop(0, PANELS)
    def _(k):
        @pl.when(k < 4)
        def _():
            plane_tail(12 + k)

        z_step(12 + k)

        @pl.when(k == 4)
        def _():
            plane_done()

        panel_step(k, mat, rows, cols)

    linv[...] = jnp.where(rows >= cols, mat[...], 0.0)

    @pl.loop(0, 2048 // TILE)
    def _(t):
        z_step(12 + PANELS + t)
        lanes = pl.ds(pl.multiple_of(t * TILE, TILE), TILE)
        b1, b2, _b = split3(nn(fpt[...], fj[:, lanes]))
        l1, l2, _l = split3(linv[...])
        hi, lo = split2(nn(l1, b1) + (nn(l1, b2) + nn(l2, b1)))
        xhi[:, lanes] = hi
        xlo[:, lanes] = lo

    @pl.loop(12 + PANELS + 2048 // TILE, LAST_STEP)
    def _(t):
        z_step(t)

    total = part[z]
    for k in range(1, 8):
        rs_copy(k).wait_recv()
        total = total + inbox[k]
    sc[...] = total * (1.0 / math.sqrt(P_SIZE))

    @pl.when(d == 0)
    def _():
        fi_own.wait()

    fp_half.wait_send()

    @pl.when(w == 0)
    def _():
        @pl.loop(1, 16)
        def _(k):
            dcopy(k).wait_send()

    @pl.when(c == 0)
    def _():
        d_across.wait_send()

    @pl.when(z == 0)
    def _():
        for k in range(1, 8):
            fpz(k).wait_send()

    @pl.loop(1, 16)
    def _(k):
        fp_direct(k).wait_send()

    @pl.loop(1, 8)
    def _(k):
        rs_copy(k).wait_send()

    for op in sends:
        op.wait_send()

    @pl.loop(12, 16)
    def _(p):
        ref = fj.at[pl.ds(z_rows(p, 0), 32), :]
        rcopy(ref, ref, pt_send.at[p], pt_recv.at[p], partner).wait_send()

    @pl.loop(0, 16)
    def _(p):
        one_way = p < RELAYED

        @pl.when(one_way & (d < 7))
        def _():
            z_copy(p, 0, False, up, 0).wait_send()

        @pl.when(one_way & (d != 1))
        def _():
            z_copy(p, 1, False, down, 1).wait_send()

        for s in range(2):
            @pl.when(jnp.logical_not(one_way) & (d < 4))
            def _():
                z_copy(p, s, False, up, 0).wait_send()

            @pl.when(jnp.logical_not(one_way) & ((d > 5) | (d == 0)))
            def _():
                z_copy(p, s, False, down, 1).wait_send()


def gather(features, queries, damping):
    vmem = pl.BlockSpec(memory_space=pltpu.VMEM)
    hbm = pl.BlockSpec(memory_space=pltpu.HBM)
    dma = pltpu.SemaphoreType.DMA
    return pl.pallas_call(
        gather_kernel,
        name="gather",
        out_shape=[
            jax.ShapeDtypeStruct((SLAB, 2048), BF16),
            jax.ShapeDtypeStruct((SLAB, 512), BF16),
            jax.ShapeDtypeStruct((SLAB, PIV), BF16),
            jax.ShapeDtypeStruct((PIV, PIV), F32),
            jax.ShapeDtypeStruct((PIV, 2048), BF16),
            jax.ShapeDtypeStruct((PIV, 2048), BF16),
            jax.ShapeDtypeStruct((64, 128), F32),
        ],
        in_specs=[hbm] * 3,
        out_specs=[vmem] * 7,
        scratch_shapes=[
            pltpu.VMEM((64, 2048), BF16),
            pltpu.VMEM((4, 128), F32),
            pltpu.VMEM((PIV, SLAB), BF16),
            pltpu.VMEM((PIV, PIV), F32),
            pltpu.VMEM((8, 64, 128), F32),
            pltpu.VMEM((8, 64, 128), F32),
            dma((32,)), dma((40,)), dma((16,)), dma((16,)), dma((32,)), dma((64,)), dma(()), dma((8,)),
            dma((16,)), dma((16,)), dma(()), dma(()), dma(()), dma((17,)), dma((8,)), dma((8,)), dma((5,)),
        ],
        compiler_params=pltpu.CompilerParams(
            collective_id=0, has_side_effects=True, vmem_limit_bytes=40 * 1024 * 1024
        ),
    )(*(pltpu.with_memory_space_constraint(v, pltpu.HBM) for v in (features, queries, damping)))


def final_kernel(fj, xhi, xlo, fi, fp, linv, damp, sc, kout, fout, sout, fit, xcat):
    w = lax.axis_index("wide")
    z = lax.axis_index("narrow")
    t = pl.program_id(0)

    @pl.when(t == 0)
    def _():
        fit[...] = (fi[...] * jnp.asarray(1.0 / SLAB, BF16)).T
        a = nn(fit[...], fp[...])
        row = w * 512 + lax.broadcasted_iota(jnp.int32, (512, PIV), 0)
        col = lax.broadcasted_iota(jnp.int32, (512, PIV), 1)
        lanes = jnp.concatenate([damp[0:1, :], damp[1:2, :]], axis=1)
        a = a + jnp.where(row == col, lanes, 0.0)
        a1, a2, a3 = split3(a)
        l1, l2, l3 = split3(linv[...])
        xrow = (
            nt(a1, l1) + (nt(a1, l2) + nt(a2, l1)) + (nt(a1, l3) + nt(a2, l2) + nt(a3, l1))
        )
        xrow = jnp.where((row < 128) & (col >= 128), 0.0, xrow)
        fout[...] = xrow
        hi, lo = split2(xrow)
        xcat[:, 0:256] = -hi
        xcat[:, 256:512] = -hi
        xcat[:, 512:768] = -lo
        sout[...] = sc[...]

    k = nn(fit[...], fj[...]) + nn(xcat[...], jnp.concatenate([xhi[...], xlo[...], xhi[...]], axis=0))
    row = lax.broadcasted_iota(jnp.int32, (512, TILE), 0)
    lane = lax.broadcasted_iota(jnp.int32, (512, TILE), 1)
    col = z * 2048 + t * TILE
    lanes = jnp.concatenate([damp[i : i + 1, :] for i in range(4)], axis=1)
    k = k + jnp.where((row == lane) & (col == w * 512), lanes, 0.0)
    kout[...] = jnp.where((w * 512 + row < PIV) | (col + lane < PIV), 0.0, k)


def finish(fj, fi, fp, linv, xhi, xlo, sc, damping):
    def whole(shape):
        return pl.BlockSpec(shape, lambda t: (0,) * len(shape))

    def tiled(rows):
        return pl.BlockSpec((rows, TILE), lambda t: (0, t))

    return pl.pallas_call(
        final_kernel,
        name="finish",
        grid=(2048 // TILE,),
        out_shape=[
            jax.ShapeDtypeStruct((512, 2048), F32),
            jax.ShapeDtypeStruct((512, PIV), F32),
            jax.ShapeDtypeStruct((64, 128), F32),
        ],
        in_specs=[
            tiled(SLAB), tiled(PIV), tiled(PIV),
            whole((SLAB, 512)), whole((SLAB, PIV)), whole((PIV, PIV)), whole((4, 128)), whole((64, 128)),
        ],
        out_specs=[tiled(512), whole((512, PIV)), whole((64, 128))],
        scratch_shapes=[
            pltpu.VMEM((512, SLAB), BF16),
            pltpu.VMEM((512, 768), BF16),
        ],
        compiler_params=pltpu.CompilerParams(vmem_limit_bytes=40 * 1024 * 1024),
    )(fj, xhi, xlo, fi, fp, linv, damping, sc)


def on_device(features, queries, damping):
    damping = damping.reshape(4, 128)
    return tuple(finish(*gather(features, queries, damping), pltpu.with_memory_space_constraint(damping, pltpu.HBM)))


def solution(mesh):
    return jax.shard_map(
        on_device,
        mesh=mesh,
        in_specs=(P("wide", "narrow"), P("wide", "narrow"), P("wide")),
        out_specs=(P("wide", "narrow"), P("wide", None), P("wide", "narrow")),
        check_vma=False,
    )
```

```python
import functools
import math

import jax
import jax.numpy as jnp
from jax import lax
from jax.experimental import pallas as pl
from jax.experimental.pallas import tpu as pltpu
from jax.sharding import PartitionSpec as P

P_SIZE = 16384
PIV = 256
SLAB = 1024
MESH = pl.DeviceIdType.MESH
F32 = jnp.float32
BF16 = jnp.bfloat16

ORDER = (
    (0, 0), (3, 0), (1, 0), (0, 3), (0, 1), (2, 0), (3, 3), (1, 3),
    (3, 1), (1, 1), (2, 3), (2, 1), (0, 2), (3, 2), (1, 2), (2, 2),
)
RELAYED = 6
LAG = 3
LAST_STEP = max(RELAYED + 7 * LAG if RELAYED else 0, 16 + 4 * LAG) + 1


def _table(values, p):
    out = jnp.int32(0)
    for k, v in enumerate(values):
        if v:
            out = out + jnp.where(p == k, jnp.int32(v), jnp.int32(0))
    return out


def split2(v):
    hi = v.astype(BF16)
    return hi, (v - hi.astype(F32)).astype(BF16)


def split3(v):
    hi = v.astype(BF16)
    rest = v - hi.astype(F32)
    mid = rest.astype(BF16)
    return hi, mid, (rest - mid.astype(F32)).astype(BF16)


def tn(a, b):
    return lax.dot_general(a, b, (((0,), (0,)), ((), ())), preferred_element_type=F32)


def nn(a, b):
    return lax.dot_general(a, b, (((1,), (0,)), ((), ())), preferred_element_type=F32)


def nt(a, b):
    return lax.dot_general(a, b, (((1,), (1,)), ((), ())), preferred_element_type=F32)


WIDTH = 32
PANELS = PIV // WIDTH
TILE = 512


def panel_step(k, mat, rows, cols):
    row_w = lax.broadcasted_iota(jnp.int32, (WIDTH, 1), 0)
    lane_w = lax.broadcasted_iota(jnp.int32, (WIDTH, PIV), 1)
    aug = jnp.where(
        lax.broadcasted_iota(jnp.int32, (WIDTH, 128), 0) == lax.broadcasted_iota(jnp.int32, (WIDTH, 128), 1),
        jnp.float32(1.0), jnp.float32(0.0),
    )
    c0 = pl.multiple_of(k * WIDTH, WIDTH)
    r = pltpu.roll(mat[pl.ds(c0, WIDTH), :], lax.rem(PIV - c0, PIV), 1)
    scale = jnp.zeros((WIDTH, 1), F32)
    for j0 in range(0, WIDTH, 8):
        column = [jnp.broadcast_to(r[:, j0 + t : j0 + t + 1], (WIDTH, 128)) for t in range(8)]
        for t in range(8):
            j = j0 + t
            pivot = column[t][j : j + 1, :]
            scale = scale + jnp.where(row_w == j, pivot[:, 0:1], 0.0)
            m = jnp.where(row_w > j, column[t] * (1.0 / pivot), 0.0)
            for u in range(t + 1, 8):
                column[u] = column[u] - m * column[u][j : j + 1, :]
            r = r - jnp.concatenate([m, m], axis=1) * r[j : j + 1, :]
            aug = aug - m * aug[j : j + 1, :]
    s = lax.rsqrt(scale)
    s = s * (1.5 - 0.5 * scale * s * s)
    r = r * s
    aug = aug * s
    r = pltpu.roll(r, c0, 1)
    aug = pltpu.roll(jnp.concatenate([aug, jnp.zeros((WIDTH, 128), F32)], axis=1), c0, 1)
    inside = (lane_w >= c0) & (lane_w < c0 + WIDTH)
    v = jnp.where(inside, aug, r)
    mat[pl.ds(c0, WIDTH), :] = v
    below = jnp.where(lane_w >= c0 + WIDTH, r, 0.0)
    a1, a2, a3 = split3(below)
    b1, b2, b3 = split3(v)
    lhs = jnp.concatenate([a1, a1, a2, a1, a2, a3], axis=0)
    rhs = jnp.concatenate([b1, b2, b1, b3, b2, b1], axis=0)
    change = tn(lhs, rhs)
    fresh = (cols >= c0) & (cols < c0 + WIDTH) & (rows >= c0 + WIDTH)
    mat[...] = jnp.where(fresh, 0.0, mat[...]) - change


def gather_kernel(
    feat, qry_hbm, damp, fj, fi, fp, linv, xhi, xlo, sc,
    qry, dp, fpt, mat, part, inbox,
    ag_recv, ag_send, pt_recv, pt_send, z_recv, z_send, fpz_recv, fpz_send,
    fp_recv, fp_send, fpp_recv, fpp_send, d_recv, d_send, rs_recv, rs_send, local,
):
    w = lax.axis_index("wide")
    z = lax.axis_index("narrow")
    c = lax.rem(w, 2)
    x = lax.rem(lax.div(w, 2), 4)
    y = lax.div(w, 8)

    def spot(da, db, core):
        px = lax.rem(x + da + core * (db - da), 4)
        py = lax.rem(y + db + core * (da - db), 4)
        return px, py

    def dev(da, db):
        px, py = spot(da, db, c)
        return ((py * 4 + px) * 2 + c, z)

    def row(da, db, core):
        px, py = spot(da, db, core)
        return pl.multiple_of((core * 16 + py * 4 + px) * 32, 32)

    partner = (w + 1 - 2 * c, z)
    own = row(0, 0, c)

    def rcopy(src, dst, ssem, rsem, to):
        return pltpu.make_async_remote_copy(
            src_ref=src, dst_ref=dst, send_sem=ssem, recv_sem=rsem, device_id=to, device_id_type=MESH
        )

    fj_own = pltpu.make_async_copy(feat, fj.at[pl.ds(own, 32), :], local.at[1])
    fj_own.start()
    qry_copy = pltpu.make_async_copy(qry_hbm, qry, local.at[2])
    qry_copy.start()
    dp_own = pltpu.make_async_copy(damp, dp, local.at[4])

    @pl.when(w == 0)
    def _():
        dp_own.start()

    barrier = pltpu.get_barrier_semaphore()

    @pl.loop(1, 16)
    def _(k):
        pl.semaphore_signal(
            barrier, inc=1, device_id=dev(lax.div(k, 4), lax.rem(k, 4)), device_id_type=MESH
        )

    @pl.loop(1, 8)
    def _(k):
        pl.semaphore_signal(barrier, inc=1, device_id=(w, lax.rem(z + k, 8)), device_id_type=MESH)

    pl.semaphore_signal(barrier, inc=1, device_id=partner, device_id_type=MESH)
    fj_own.wait()
    pl.semaphore_wait(barrier, 23)

    def fpz(k):
        return rcopy(
            fj.at[pl.ds(own, 32), pl.ds(0, PIV)], fp.at[pl.ds(own, 32), :], fpz_send.at[k], fpz_recv,
            (w, lax.rem(z + k, 8)),
        )

    fp_own = pltpu.make_async_copy(
        fj.at[pl.ds(own, 32), pl.ds(0, PIV)], fp.at[pl.ds(own, 32), :], local.at[0]
    )

    def dcopy(k):
        return rcopy(dp, dp, d_send.at[k], d_recv, dev(lax.div(k, 4), lax.rem(k, 4)))

    d_across = rcopy(dp, dp, d_send.at[16], d_recv, partner)

    @pl.when(z == 0)
    def _():
        for k in (4, 3, 5, 2, 6, 1, 7):
            fpz(k).start()
        fp_own.start()

    @pl.when(w == 0)
    def _():
        dp_own.wait()

        @pl.loop(1, 16)
        def _(k):
            dcopy(k).start()


    sends = []

    def send_block(da, db, half, to, as_da, as_db):
        n = len(sends)
        r = row(da, db, c)
        if half is None:
            rows, index = pl.ds(r, 32), (as_da * 4 + as_db) * 2
        else:
            rows, index = pl.ds(r + 16 * half, 16), (as_da * 4 + as_db) * 2 + half
        op = rcopy(
            fj.at[rows, :], fj.at[rows, :],
            ag_send.at[n], ag_recv.at[index], to,
        )
        op.start()
        sends.append(op)

    def wait_block(da, db):
        r = row(da, db, c)
        base = (da * 4 + db) * 2
        if da == 2 and db == 0 or db == 2:
            for h in range(2):
                ref = fj.at[pl.ds(r + 16 * h, 16), :]
                rcopy(ref, ref, ag_send.at[0], ag_recv.at[base + h], partner).wait_recv()
        else:
            ref = fj.at[pl.ds(r, 32), :]
            rcopy(ref, ref, ag_send.at[0], ag_recv.at[base], partner).wait_recv()

    def to_partner(p):
        da, db = ORDER[p]
        ref = fj.at[pl.ds(row(da, db, c), 32), :]
        op = rcopy(ref, ref, pt_send.at[p], pt_recv.at[p], partner)
        op.start()
        sends.append(op)

    def plane_event(p):
        da, db = ORDER[p]
        if p:
            wait_block(da, db)
        if db == 0:
            if da == 0:
                send_block(0, 0, None, dev(1, 0), 3, 0)
                send_block(0, 0, None, dev(3, 0), 1, 0)
            elif da == 3:
                send_block(3, 0, 0, dev(1, 0), 2, 0)
            elif da == 1:
                send_block(1, 0, 1, dev(3, 0), 2, 0)
            send_block(da, 0, None, dev(0, 1), da, 3)
            send_block(da, 0, None, dev(0, 3), da, 1)
        elif db == 3:
            send_block(da, 3, 0, dev(0, 1), da, 2)
        elif db == 1:
            send_block(da, 1, 1, dev(0, 3), da, 2)
        to_partner(p)

    def fp_direct(k):
        da, db = lax.div(k, 4), lax.rem(k, 4)
        back = lax.rem(4 - da, 4) * 4 + lax.rem(4 - db, 4)
        ref = fp.at[pl.ds(own, 32), :]
        return rcopy(ref, ref, fp_send.at[k], fp_recv.at[back], dev(da, db))

    half_rows = fp.at[pl.ds(pl.multiple_of(c * 512, 512), 512), :]
    fp_half = rcopy(half_rows, half_rows, fpp_send, fpp_recv, partner)

    def panel_start():
        @pl.when(z == 0)
        def _():
            fp_own.wait()

        @pl.when(z != 0)
        def _():
            fpz(0).wait_recv()

        @pl.loop(1, 16)
        def _(k):
            fp_direct(k).start()

    def panel_to_partner():
        @pl.loop(1, 16)
        def _(k):
            fp_direct(k).wait_recv()

        fp_half.start()

        @pl.when(c == 0)
        def _():
            @pl.when(w != 0)
            def _():
                dcopy(0).wait_recv()

            d_across.start()

    home = lax.div(w, 4)
    d = lax.rem(z - home + 8, 8)
    sub = pl.multiple_of(lax.rem(w, 4) * 512, 512)
    up = (w, lax.rem(z + 1, 8))
    down = (w, lax.rem(z + 7, 8))
    hops_up = d
    hops_down = lax.rem(8 - d, 8)
    near = jnp.minimum(hops_up, hops_down)

    def z_rows(p, s):
        da = _table([o[0] for o in ORDER], p)
        db = _table([o[1] for o in ORDER], p)
        core = c if s == 0 else 1 - c
        return row(da, db, core)

    def z_copy(p, s, from_root, to, way):
        r = z_rows(p, s)
        dst = fi.at[pl.ds(r, 32), :]
        src = fj.at[pl.ds(r, 32), pl.ds(sub, 512)] if from_root else dst
        q = p * 2 + s
        return rcopy(src, dst, z_send.at[q * 2 + way], z_recv.at[q], to)

    def pt_wait(p):
        ref = fj.at[pl.ds(z_rows(p, 1), 32), :]
        rcopy(ref, ref, pt_send.at[0], pt_recv.at[p], partner).wait_recv()

    def z_step(t):
        first = t - 1

        @pl.when((d == 0) & (first >= 0) & (first < RELAYED))
        def _():
            z_copy(first, 0, True, up, 0).start()
            pt_wait(first)
            z_copy(first, 1, True, down, 1).start()

        @pl.when((d == 0) & (first >= RELAYED) & (first < 16))
        def _():
            z_copy(first, 0, True, up, 0).start()
            z_copy(first, 0, True, down, 1).start()
            pt_wait(first)
            z_copy(first, 1, True, up, 0).start()
            z_copy(first, 1, True, down, 1).start()

        pu = first - LAG * hops_up

        @pl.when((d != 0) & (pu >= 0) & (pu < RELAYED))
        def _():
            z_copy(pu, 0, False, up, 0).wait_recv()

            @pl.when(d < 7)
            def _():
                z_copy(pu, 0, False, up, 0).start()

        pd = first - LAG * hops_down

        @pl.when((d != 0) & (pd >= 0) & (pd < RELAYED))
        def _():
            z_copy(pd, 1, False, down, 1).wait_recv()

            @pl.when(d > 1)
            def _():
                z_copy(pd, 1, False, down, 1).start()

        pn = first - LAG * near

        @pl.when((d != 0) & (pn >= RELAYED) & (pn < 16))
        def _():
            for s in range(2):
                z_copy(pn, s, False, up, 0).wait_recv()

                @pl.when(d < 4)
                def _():
                    z_copy(pn, s, False, up, 0).start()

                @pl.when(d > 5)
                def _():
                    z_copy(pn, s, False, down, 1).start()

    def plane_tail(p):
        r = z_rows(p, 0)
        da = _table([o[0] for o in ORDER], p)
        for h in range(2):
            ref = fj.at[pl.ds(r + 16 * h, 16), :]
            rcopy(ref, ref, ag_send.at[0], ag_recv.at[(da * 4 + 2) * 2 + h], partner).wait_recv()
        ref = fj.at[pl.ds(r, 32), :]
        rcopy(ref, ref, pt_send.at[p], pt_recv.at[p], partner).start()

    fi_own = pltpu.make_async_copy(fj.at[:, pl.ds(sub, 512)], fi, local.at[3])

    def scores_for(k):
        yk = lax.div(k, 2)
        xk = lax.rem(k, 2) * 2
        pieces = []
        for dx in range(2):
            for core in range(2):
                r = pl.multiple_of((core * 16 + yk * 4 + xk + dx) * 32, 32)
                pieces.append(fj[pl.ds(r, 32), :])
        return lax.dot_general(
            qry[...], jnp.concatenate(pieces, axis=0), (((1,), (1,)), ((), ())),
            preferred_element_type=F32,
        )

    def rs_copy(k):
        to = lax.rem(z + k, 8)
        return rcopy(part.at[to], inbox.at[k], rs_send.at[k], rs_recv.at[k], (w, to))

    def plane_done():
        @pl.when(d != 0)
        def _():
            @pl.loop(0, 16)
            def _(p):
                pt_wait(p)

        @pl.when(d == 0)
        def _():
            fi_own.start()

        qry_copy.wait()

    for t in range(12):
        plane_event(t)
        if t == 4:
            panel_start()
        if t == 9:
            panel_to_partner()
        z_step(jnp.int32(t))

    fp_half.wait_recv()

    @pl.when(c != 0)
    def _():
        d_across.wait_recv()

    rows = lax.broadcasted_iota(jnp.int32, (PIV, PIV), 0)
    cols = lax.broadcasted_iota(jnp.int32, (PIV, PIV), 1)
    diag = jnp.concatenate([dp[0:1, :], dp[1:2, :]], axis=1)
    fpt[...] = (fp[...] * jnp.asarray(1.0 / SLAB, BF16)).T
    mat[...] = nn(fpt[...], fp[...]) + jnp.where(rows == cols, diag, 0.0)

    @pl.loop(0, PANELS)
    def _(k):
        @pl.when(k < 4)
        def _():
            plane_tail(12 + k)

        z_step(12 + k)

        @pl.when(k == 4)
        def _():
            plane_done()

        @pl.when(k >= 4)
        def _():
            @pl.loop(2 * k - 7, 2 * k - 5)
            def _(q):
                part[lax.rem(z + q, 8)] = scores_for(lax.rem(z + q, 8))

                @pl.when(q < 8)
                def _():
                    rs_copy(q).start()

        panel_step(k, mat, rows, cols)

    linv[...] = jnp.where(rows >= cols, mat[...], 0.0)

    @pl.loop(0, 2048 // TILE)
    def _(t):
        z_step(12 + PANELS + t)
        lanes = pl.ds(pl.multiple_of(t * TILE, TILE), TILE)
        b1, b2, _b = split3(nn(fpt[...], fj[:, lanes]))
        l1, l2, _l = split3(linv[...])
        hi, lo = split2(nn(l1, b1) + (nn(l1, b2) + nn(l2, b1)))
        xhi[:, lanes] = hi
        xlo[:, lanes] = lo

    @pl.loop(12 + PANELS + 2048 // TILE, LAST_STEP)
    def _(t):
        z_step(t)

    total = part[z]
    for k in range(1, 8):
        rs_copy(k).wait_recv()
        total = total + inbox[k]
    sc[...] = total * (1.0 / math.sqrt(P_SIZE))

    @pl.when(d == 0)
    def _():
        fi_own.wait()

    fp_half.wait_send()

    @pl.when(w == 0)
    def _():
        @pl.loop(1, 16)
        def _(k):
            dcopy(k).wait_send()

    @pl.when(c == 0)
    def _():
        d_across.wait_send()

    @pl.when(z == 0)
    def _():
        for k in range(1, 8):
            fpz(k).wait_send()

    @pl.loop(1, 16)
    def _(k):
        fp_direct(k).wait_send()

    @pl.loop(1, 8)
    def _(k):
        rs_copy(k).wait_send()

    for op in sends:
        op.wait_send()

    @pl.loop(12, 16)
    def _(p):
        ref = fj.at[pl.ds(z_rows(p, 0), 32), :]
        rcopy(ref, ref, pt_send.at[p], pt_recv.at[p], partner).wait_send()

    @pl.loop(0, 16)
    def _(p):
        one_way = p < RELAYED

        @pl.when(one_way & (d < 7))
        def _():
            z_copy(p, 0, False, up, 0).wait_send()

        @pl.when(one_way & (d != 1))
        def _():
            z_copy(p, 1, False, down, 1).wait_send()

        for s in range(2):
            @pl.when(jnp.logical_not(one_way) & (d < 4))
            def _():
                z_copy(p, s, False, up, 0).wait_send()

            @pl.when(jnp.logical_not(one_way) & ((d > 5) | (d == 0)))
            def _():
                z_copy(p, s, False, down, 1).wait_send()


def gather(features, queries, damping):
    vmem = pl.BlockSpec(memory_space=pltpu.VMEM)
    hbm = pl.BlockSpec(memory_space=pltpu.HBM)
    dma = pltpu.SemaphoreType.DMA
    return pl.pallas_call(
        gather_kernel,
        name="gather",
        out_shape=[
            jax.ShapeDtypeStruct((SLAB, 2048), BF16),
            jax.ShapeDtypeStruct((SLAB, 512), BF16),
            jax.ShapeDtypeStruct((SLAB, PIV), BF16),
            jax.ShapeDtypeStruct((PIV, PIV), F32),
            jax.ShapeDtypeStruct((PIV, 2048), BF16),
            jax.ShapeDtypeStruct((PIV, 2048), BF16),
            jax.ShapeDtypeStruct((64, 128), F32),
        ],
        in_specs=[hbm] * 3,
        out_specs=[vmem] * 7,
        scratch_shapes=[
            pltpu.VMEM((64, 2048), BF16),
            pltpu.VMEM((4, 128), F32),
            pltpu.VMEM((PIV, SLAB), BF16),
            pltpu.VMEM((PIV, PIV), F32),
            pltpu.VMEM((8, 64, 128), F32),
            pltpu.VMEM((8, 64, 128), F32),
            dma((32,)), dma((40,)), dma((16,)), dma((16,)), dma((32,)), dma((64,)), dma(()), dma((8,)),
            dma((16,)), dma((16,)), dma(()), dma(()), dma(()), dma((17,)), dma((8,)), dma((8,)), dma((5,)),
        ],
        compiler_params=pltpu.CompilerParams(
            collective_id=0, has_side_effects=True, vmem_limit_bytes=40 * 1024 * 1024
        ),
    )(*(pltpu.with_memory_space_constraint(v, pltpu.HBM) for v in (features, queries, damping)))


FINISH_TILE = 512


def final_kernel(fj, xhi, xlo, fi, fp, linv, damp, sc, kout, fout, sout, fit, xcat):
    w = lax.axis_index("wide")
    z = lax.axis_index("narrow")
    t = pl.program_id(0)

    @pl.when(t == 0)
    def _():
        fit[...] = (fi[...] * jnp.asarray(1.0 / SLAB, BF16)).T
        a = nn(fit[...], fp[...])
        row = w * 512 + lax.broadcasted_iota(jnp.int32, (512, PIV), 0)
        col = lax.broadcasted_iota(jnp.int32, (512, PIV), 1)
        lanes = jnp.concatenate([damp[0:1, :], damp[1:2, :]], axis=1)
        a = a + jnp.where(row == col, lanes, 0.0)
        a1, a2, a3 = split3(a)
        l1, l2, l3 = split3(linv[...])
        xrow = (
            nt(a1, l1) + (nt(a1, l2) + nt(a2, l1)) + (nt(a1, l3) + nt(a2, l2) + nt(a3, l1))
        )
        xrow = jnp.where((row < 128) & (col >= 128), 0.0, xrow)
        fout[...] = xrow
        hi, lo = split2(xrow)
        xcat[:, 0:256] = -hi
        xcat[:, 256:512] = -hi
        xcat[:, 512:768] = -lo
        sout[...] = sc[...]

    tile = pl.ds(pl.multiple_of(t * FINISH_TILE, FINISH_TILE), FINISH_TILE)
    xh = xhi[:, tile]
    k = nn(fit[...], fj[:, tile]) + nn(xcat[...], jnp.concatenate([xh, xlo[:, tile], xh], axis=0))
    row = w * 512 + lax.broadcasted_iota(jnp.int32, (512, FINISH_TILE), 0)
    col = z * 2048 + t * FINISH_TILE + lax.broadcasted_iota(jnp.int32, (512, FINISH_TILE), 1)
    kout[...] = jnp.where((row < PIV) | (col < PIV), 0.0, k)

    gap = w * 512 - (z * 2048 + t * FINISH_TILE)
    for part in range(4):
        at = gap + part * 128

        @pl.when((at >= 0) & (at < FINISH_TILE) & (w * 512 + part * 128 >= PIV))
        def _():
            square = kout[part * 128 : part * 128 + 128, pl.ds(pl.multiple_of(at, 128), 128)]
            on = lax.broadcasted_iota(jnp.int32, (128, 128), 0) == lax.broadcasted_iota(jnp.int32, (128, 128), 1)
            kout[part * 128 : part * 128 + 128, pl.ds(pl.multiple_of(at, 128), 128)] = square + jnp.where(
                on, damp[part : part + 1, :], 0.0
            )


def finish(fj, fi, fp, linv, xhi, xlo, sc, damping):
    vmem = pl.BlockSpec(memory_space=pltpu.VMEM)

    def whole(shape):
        return pl.BlockSpec(shape, lambda t: (0,) * len(shape))

    return pl.pallas_call(
        final_kernel,
        name="finish",
        grid=(2048 // FINISH_TILE,),
        out_shape=[
            jax.ShapeDtypeStruct((512, 2048), F32),
            jax.ShapeDtypeStruct((512, PIV), F32),
            jax.ShapeDtypeStruct((64, 128), F32),
        ],
        in_specs=[vmem] * 8,
        out_specs=[
            pl.BlockSpec((512, FINISH_TILE), lambda t: (0, t)), whole((512, PIV)), whole((64, 128)),
        ],
        scratch_shapes=[
            pltpu.VMEM((512, SLAB), BF16),
            pltpu.VMEM((512, 768), BF16),
        ],
        compiler_params=pltpu.CompilerParams(vmem_limit_bytes=40 * 1024 * 1024),
    )(fj, xhi, xlo, fi, fp, linv, damping, sc)


def on_device(features, queries, damping):
    damping = damping.reshape(4, 128)
    return tuple(finish(*gather(features, queries, damping), pltpu.with_memory_space_constraint(damping, pltpu.HBM)))


def solution(mesh):
    return jax.shard_map(
        on_device,
        mesh=mesh,
        in_specs=(P("wide", "narrow"), P("wide", "narrow"), P("wide")),
        out_specs=(P("wide", "narrow"), P("wide", None), P("wide", "narrow")),
        check_vma=False,
    )
```
